32 devices in a mesh: scene: 2 (over y), aper: 8 (over z, x), range: 2 (over core).
Axes of the slice: x: 2, y: 2, z: 4, core: 2. Of those that a mesh axis runs over, the one named last changes fastest.
Arguments:
- images: bfloat16 [16, 2, 512, 256], P(('scene', 'aper'), None, None, 'range'), parts along dimension 0, may hold values from -6 to 6
- interp_matrix: bfloat16 [1024, 512], replicated, may hold values from -0.25 to 0.25
- offsets: int32 [3, 2, 1024], replicated, may hold values from -28 to 28, as said below
- tap_index: int32 [3, 2, 1024], replicated, may hold values from 0 to 15
- tap_table: float32 [16, 8], replicated, may hold values from -1.5 to 1.5
- phase_base: float32 [3, 2, 1024], replicated, may hold values from -3.140625 to 3.140625
- phase_slope: float32 [3, 2, 1024], replicated, may hold values from -0.5 to 0.5
Outputs:
- merged: bfloat16 [16, 2, 512, 256], P(('scene', 'aper'), None, None, 'range'), parts along dimension 0
The draws below stay inside these ranges and needn't reach their ends.
There are 2 independent parts, one for each index of `scene`. The reference program is written for one: setup_inputs(seed, part) draws one part's arguments, and reference() takes and returns one part's arrays. A program takes and returns all parts, laid end to end along the dimension named above; an argument that names none is the same for every part. Nothing has to cross between parts.
Inputs may be any that keep to these rules, and one draw needn't show every extreme that they name: `offsets`: for every level and role both -28 and 28 occur.
All inputs are finite; a program needn't handle non-finite values.
Results may differ from the reference program's by a relative error of at most 0.0085.
Values may be sent and summed in bfloat16 or wider, within the bound.
A program may use at most 64 MiB of HBM per device.

```python
from functools import partial
import jax
import jax.numpy as jnp
from jax import lax

ANG = 512
LEVELS = 3
HALO = 32
MAXOFF = 28
NFRAC = 16
TAPS = 8
APERS = 8
RANGE = 256
PARENT = 1024


def draw_offsets(key, part):
    values = jax.random.randint(jax.random.fold_in(key, 17), (LEVELS, 2, PARENT), -MAXOFF, MAXOFF + 1, dtype=jnp.int32)
    values = values.at[:, :, 0].set(-MAXOFF)
    values = values.at[:, :, 1].set(MAXOFF)
    return values


def plant(values, rng, smallest, high):
    longest = values.shape.index(max(values.shape))
    spots = []
    for shift in (0, 1):
        where = [jax.random.randint(jax.random.fold_in(rng, axis), (), 0, length) for axis, length in enumerate(values.shape)]
        where[longest] = (where[longest] + shift) % values.shape[longest]
        spots.append(tuple(where))
    return values.at[spots[0]].set(smallest).at[spots[1]].set(high)


def levels(own_key, extent, pieces, low, high):
    def one(axis_at, parts):
        steps = jax.random.uniform(jax.random.fold_in(jax.random.fold_in(own_key, 6), axis_at), (parts,), jnp.float32, low / len(pieces), high / len(pieces))
        return jnp.repeat(jnp.exp(steps), extent[axis_at] // parts).reshape((-1,) + (1,) * (len(extent) - axis_at - 1))

    factor_of = one(*pieces[0])
    for cut in pieces[1:]:
        factor_of = factor_of * one(*cut)
    return factor_of


def scatter_about(stream_key, dims, deviation, bound, cuts=(), held_as=jnp.bfloat16):
    array = jax.random.normal(stream_key, dims, jnp.float32) * deviation
    if len(cuts) > 0:
        array = levels(stream_key, dims, cuts, -0.22, 0.18) * array
    return jnp.clip(array, min=-bound, max=bound).astype(held_as)


def setup_inputs(seed: int = 0, part: int = 0) -> dict:
    key_list = jax.random.split(jax.random.key(seed), 8)
    own_keys = jax.random.split(jax.random.fold_in(key_list[7], part), 8)
    images = scatter_about(own_keys[0], (APERS, 2, ANG, RANGE), 1.0, 6.0, ((0, 8), (3, 2)))
    interp_matrix = scatter_about(key_list[1], (PARENT, ANG), ANG ** -0.5, 0.25)
    offsets = draw_offsets(jax.random.fold_in(key_list[7], 71), part)
    tap_index = plant(jax.random.randint(key_list[3], (LEVELS, 2, PARENT), 0, NFRAC), jax.random.fold_in(key_list[3], 1), 0, NFRAC - 1).astype(jnp.int32)
    tap_table = scatter_about(key_list[4], (NFRAC, TAPS), 0.25, 1.5, (), jnp.float32)
    phase_base = jnp.clip(jax.random.uniform(key_list[5], (LEVELS, 2, PARENT), jnp.float32, -3.140625, 3.140625), -3.140625, 3.140625)
    phase_slope = jnp.clip(jax.random.uniform(key_list[6], (LEVELS, 2, PARENT), jnp.float32, -0.5, 0.5), -0.5, 0.5)
    return dict(images=images, interp_matrix=interp_matrix, offsets=offsets, tap_index=tap_index, tap_table=tap_table, phase_base=phase_base, phase_slope=phase_slope)


def shifted(inter, shift_rows, tap_rows, first_col, out_width):
    taps_count = tap_rows.shape[1]
    needed = out_width + taps_count - 1
    total_width = inter.shape[2]
    start_cols = (first_col - 3 + shift_rows).astype(jnp.int32)
    moved = inter
    for bit_number in range((total_width - needed).bit_length()):
        stride_len = 1 << bit_number
        rolled = jnp.concatenate([moved[:, :, stride_len:], jnp.zeros_like(moved[:, :, :stride_len])], axis=2)
        chosen_bits = ((start_cols >> bit_number) & 1) == 1
        moved = jnp.where(chosen_bits[None, :, None], rolled, moved)
    window = moved[:, :, :needed]
    summed = jnp.zeros(window.shape[:2] + (out_width,), jnp.float32)
    for tap_number in range(taps_count):
        summed = summed + tap_rows[None, :, tap_number, None] * window[:, :, tap_number:tap_number + out_width].astype(jnp.float32)
    return summed


def child_term(inter, merge_level, child_role, offsets, tap_index, tap_table, phase_base, phase_slope):
    padded = jnp.pad(inter, ((0, 0), (0, 0), (HALO, HALO)))
    onehot = (tap_index[merge_level, child_role][:, None] == jnp.arange(NFRAC, dtype=jnp.int32)[None, :]).astype(jnp.float32)
    tap_rows = jnp.dot(onehot, tap_table, precision=lax.Precision.HIGHEST, preferred_element_type=jnp.float32)
    summed = shifted(padded, offsets[merge_level, child_role], tap_rows, HALO, RANGE)
    positions = jnp.arange(RANGE).astype(jnp.float32)
    phase_angle = phase_base[merge_level, child_role][:, None] + phase_slope[merge_level, child_role][:, None] * positions[None, :]
    cosine = jnp.cos(phase_angle)
    sine_part = jnp.sin(phase_angle)
    real_part = summed[0]
    imag_part = summed[1]
    return jnp.stack([real_part * cosine - imag_part * sine_part, real_part * sine_part + imag_part * cosine])


def merge_pair(merge_level, interp_matrix, offsets, tap_index, tap_table, phase_base, phase_slope, children):
    summed = jnp.zeros((2, PARENT, RANGE), jnp.float32)
    for child_role in range(2):
        inter = jnp.einsum("pa,can->cpn", interp_matrix.astype(jnp.float32), children[child_role].astype(jnp.float32),
                           precision=lax.Precision.HIGHEST).astype(jnp.bfloat16)
        summed = summed + child_term(inter, merge_level, child_role, offsets, tap_index, tap_table, phase_base, phase_slope)
    parent = summed.astype(jnp.bfloat16)
    return jnp.stack([parent[:, :ANG], parent[:, ANG:]])


def reference(images, interp_matrix, offsets, tap_index, tap_table, phase_base, phase_slope):
    current = images
    for merge_level in range(LEVELS):
        lower = 2 ** merge_level
        upper = APERS // (2 * lower)
        grouped = current.reshape(upper, 2, lower, 2, ANG, RANGE)
        pairs = jnp.transpose(grouped, (0, 2, 1, 3, 4, 5)).reshape(upper * lower, 2, 2, ANG, RANGE)
        merged = lax.map(partial(merge_pair, merge_level, interp_matrix, offsets, tap_index, tap_table, phase_base, phase_slope), pairs)
        current = jnp.transpose(merged.reshape(upper, lower, 2, 2, ANG, RANGE), (0, 2, 1, 3, 4, 5)).reshape(APERS, 2, ANG, RANGE)
    return current
```

```python
import functools

import jax
import jax.numpy as jnp
from jax import lax
from jax.experimental import pallas as pl
from jax.experimental.pallas import tpu as pltpu
from jax.sharding import PartitionSpec as P

MESH = pl.DeviceIdType.MESH
LANES = 128
REACH = 32
FINE = 8
SEND_LAGS = (0, 1, 8)
MERGE_LAGS = (0, 7, 17)
F32 = jnp.float32
BF16 = jnp.bfloat16


def sincos(angle):
    turns = jnp.floor(angle * 0.6366197723675814 + 0.5)
    rest = angle - turns * 1.5703125
    rest = rest - turns * 4.837512969970703125e-4
    rest = rest - turns * 7.54978995489188216e-8
    quadrant = turns.astype(jnp.int32)
    square = rest * rest
    sine = rest + rest * square * (
        -1.6666654611e-1 + square * (8.3321608736e-3 + square * -1.9515295891e-4)
    )
    cosine = (1.0 - 0.5 * square) + square * square * (
        4.166664568298827e-2 + square * (-1.388731625493765e-3 + square * 2.443315711809948e-5)
    )
    odd = (quadrant & 1) == 1
    swapped_sine = jnp.where(odd, cosine, sine)
    swapped_cosine = jnp.where(odd, sine, cosine)
    sine = jnp.where((quadrant & 2) == 2, -swapped_sine, swapped_sine)
    cosine = jnp.where(((quadrant + 1) & 2) == 2, -swapped_cosine, swapped_cosine)
    return sine, cosine


def kernel(
    levels,
    images_in,
    matrix,
    offsets_in,
    tap_index_in,
    tap_table,
    phase_base_in,
    phase_slope_in,
    out,
    images,
    offsets,
    tap_index,
    phase_base,
    phase_slope,
    source,
    image,
    rows_of,
    params,
    trig,
    staging,
    outgoing,
    incoming,
    kept,
    windows,
    merged,
    handed,
    local_sem,
    first_sem,
    sibling_sem,
    inter_sem,
    merge_sem,
    last_sem,
):
    width = image.shape[2]
    angles = image.shape[3]
    span = images.shape[2]
    share = rows_of.shape[1]
    cores = angles // share
    tiles = share // LANES
    steps = width // REACH
    per_owner = span // REACH
    taps = tap_table.shape[0]
    scene = lax.axis_index("scene")
    aper = lax.axis_index("aper")
    core = lax.axis_index("range")
    other = 1 - core
    first_row = pl.multiple_of(core * share, share)
    other_row = pl.multiple_of(other * share, share)
    halves = [lax.rem(aper // 2**level, 2) for level in range(levels)]
    partners = [aper + (1 - 2 * halves[level]) * 2**level for level in range(levels)]

    barrier = pltpu.get_barrier_semaphore()
    for partner in partners:
        pl.semaphore_signal(barrier, inc=1, device_id=(scene, partner, core), device_id_type=MESH)
    pl.semaphore_signal(barrier, inc=1, device_id=(scene, aper, other), device_id_type=MESH)

    pl.semaphore_signal(
        barrier, inc=1, device_id=(scene, partners[0], other), device_id_type=MESH
    )

    local_copies = [
        pltpu.make_async_copy(images_in.at[0], images, local_sem.at[0]),
        pltpu.make_async_copy(matrix, rows_of, local_sem.at[1]),
        pltpu.make_async_copy(offsets_in, offsets, local_sem.at[2]),
        pltpu.make_async_copy(tap_index_in, tap_index, local_sem.at[3]),
        pltpu.make_async_copy(phase_base_in, phase_base, local_sem.at[4]),
        pltpu.make_async_copy(phase_slope_in, phase_slope, local_sem.at[5]),
    ]
    for copy in local_copies:
        copy.start()

    def frame(step):
        return pl.ds(pl.multiple_of((step + 1) * REACH, REACH), REACH)

    def plain(step):
        return pl.ds(pl.multiple_of(step * REACH, REACH), REACH)

    def owner_of(step):
        return step // per_owner

    def local_step(step):
        return lax.rem(step, per_owner)

    def sibling_copy(step):
        return pltpu.make_async_remote_copy(
            src_ref=staging.at[0, :, plain(local_step(step)), :],
            dst_ref=kept.at[0, :, frame(step), :],
            send_sem=sibling_sem.at[0, step],
            recv_sem=sibling_sem.at[1, step],
            device_id=(scene, aper, other),
            device_id_type=MESH,
        )

    def first_copy(step, place):
        return pltpu.make_async_remote_copy(
            src_ref=staging.at[1 + place, :, plain(local_step(step)), :],
            dst_ref=incoming.at[0, :, frame(step), :],
            send_sem=first_sem.at[place, local_step(step)],
            recv_sem=inter_sem.at[1, 0, step],
            device_id=(scene, partners[0], core if place == 0 else other),
            device_id_type=MESH,
        )

    def inter_copy(level, step):
        return pltpu.make_async_remote_copy(
            src_ref=outgoing.at[level - 1, :, plain(step), :],
            dst_ref=incoming.at[level, :, frame(step), :],
            send_sem=inter_sem.at[0, level, step],
            recv_sem=inter_sem.at[1, level, step],
            device_id=(scene, partners[level], core),
            device_id_type=MESH,
        )

    def product(both, row):
        return lax.dot_general(
            both, row, (((1,), (1,)), ((), ())), preferred_element_type=F32
        ).astype(BF16)

    def first_products(j):
        step = core * per_owner + j
        both = jnp.concatenate([source[part, plain(j), :] for part in range(2)], axis=0)
        mine = halves[0] * cores
        yours = (1 - halves[0]) * cores
        for place, block in enumerate((mine + other, yours + core, yours + other)):
            inter = product(both, rows_of[block])
            for part in range(2):
                staging[place, part, plain(j), :] = inter[part * REACH : (part + 1) * REACH]
        inter = product(both, rows_of[mine + core])
        for part in range(2):
            kept[0, part, frame(step), :] = inter[part * REACH : (part + 1) * REACH]

    local_copies[0].wait()
    for part in range(2):
        source[part] = images[part].T
    local_copies[1].wait()
    first_products(0)
    edge = jnp.zeros((2, REACH, share), BF16)
    for level in range(levels):
        for buffer in (incoming, kept):
            buffer[level, :, 0:REACH, :] = edge
            buffer[level, :, REACH + width : REACH + width + REACH, :] = edge

    pl.semaphore_wait(barrier, len(partners) + 2)

    @pl.loop(0, per_owner)
    def _(j):
        step = core * per_owner + j

        @pl.when(j > 0)
        def _():
            first_products(j)

        sibling_copy(step).start()

        @pl.when(core == 0)
        def _():
            for place in range(2):
                first_copy(step, place).start()

    for copy in local_copies[2:]:
        copy.wait()

    def tables(level):
        half = halves[level]
        picked = pl.ds(pl.multiple_of(half * angles + core * share, LANES), share)
        index = tap_index[level, :, picked]
        weights = [jnp.zeros(index.shape, F32) for _ in range(taps)]
        for entry in range(tap_table.shape[1]):
            hit = index == entry
            for tap in range(taps):
                weights[tap] = jnp.where(hit, tap_table[tap, entry], weights[tap])
        base = phase_base[level, :, picked]
        slope = phase_slope[level, :, picked]
        lines = weights + [offsets[level, :, picked].astype(F32) + float(REACH - 3), base, slope]
        for row, line in enumerate(lines):
            for slot in range(2):
                role = half if slot == 0 else 1 - half
                params[level, slot, row : row + 1, :] = jnp.where(role == 0, line[0:1], line[1:2])
        for slot in range(2):
            for tile in range(tiles):
                columns = slice(tile * LANES, (tile + 1) * LANES)

                def line(row, count):
                    return jnp.broadcast_to(
                        params[level, slot, row : row + 1, columns], (count, LANES)
                    )

                fine = lax.broadcasted_iota(jnp.int32, (REACH, LANES), 0).astype(F32)
                coarse = (
                    lax.broadcasted_iota(jnp.int32, (steps, LANES), 0) * REACH
                ).astype(F32)
                near = sincos(line(taps + 2, REACH) * fine)
                far = sincos(line(taps + 1, steps) + line(taps + 2, steps) * coarse)
                for step in range(steps):
                    sine = jnp.broadcast_to(far[0][step : step + 1], (REACH, LANES))
                    cosine = jnp.broadcast_to(far[1][step : step + 1], (REACH, LANES))
                    place = pl.ds(step * REACH, REACH)
                    trig[level, slot, 0, place, columns] = sine * near[1] + cosine * near[0]
                    trig[level, slot, 1, place, columns] = cosine * near[1] - sine * near[0]

    for level in range(levels):
        tables(level)

    def merge_copy(level, step, row):
        place = image.at[
            level - 1, :, pl.ds(pl.multiple_of(step * REACH, REACH), REACH), pl.ds(row, share)
        ]
        return pltpu.make_async_remote_copy(
            src_ref=place,
            dst_ref=place,
            send_sem=merge_sem.at[0, level - 1, step],
            recv_sem=merge_sem.at[1, level - 1, step],
            device_id=(scene, aper, other),
            device_id_type=MESH,
        )

    def last_copy(row):
        return pltpu.make_async_remote_copy(
            src_ref=handed,
            dst_ref=out.at[0, :, pl.ds(row, share), :],
            send_sem=last_sem.at[0],
            recv_sem=last_sem.at[1],
            device_id=(scene, aper, other),
            device_id_type=MESH,
        )

    def send(level, step):
        merge_copy(level, step, other_row).wait_recv()
        here = plain(step)
        both = jnp.concatenate([image[level - 1, part, here, :] for part in range(2)], axis=0)
        for slot in range(2):
            half = 1 - halves[level] if slot == 0 else halves[level]
            inter = product(both, rows_of[half * cores + core])
            for part in range(2):
                piece = inter[part * REACH : (part + 1) * REACH]
                if slot == 0:
                    outgoing[level - 1, part, here, :] = piece
                else:
                    kept[level, part, frame(step), :] = piece
            if slot == 0:
                inter_copy(level, step).start()

    def term(level, slot, step, tile):
        buffer = kept if slot == 0 else incoming
        columns = slice(tile * LANES, (tile + 1) * LANES)

        def line(row, count):
            return jnp.broadcast_to(params[level, slot, row : row + 1, columns], (count, LANES))

        amount = line(taps, 2 * REACH).astype(jnp.int32)
        weights = [line(tap, REACH) for tap in range(taps)]
        sine, cosine = [trig[level, slot, which, plain(step), columns] for which in range(2)]
        shifted = []
        for part in range(2):
            value = buffer[
                level, part, pl.ds(pl.multiple_of(step * REACH, REACH), 3 * REACH), columns
            ].astype(F32)
            keep = 2 * REACH
            bit = REACH
            value = jnp.concatenate(
                [
                    jnp.where((amount & bit) == bit, value[bit:], value[:keep]),
                    value[keep : keep + FINE],
                ],
                axis=0,
            )
            while bit > FINE:
                bit //= 2
                keep = value.shape[0] - bit
                value = jnp.where((amount[:keep] & bit) == bit, value[bit:], value[:keep])
            while bit > 1:
                bit //= 2
                turned = pltpu.roll(value, value.shape[0] - bit, 0)
                value = jnp.where((amount[: value.shape[0]] & bit) == bit, turned, value)
            window = windows.at[tile, slot, part]
            window[...] = value
            total = weights[0] * value[:REACH]
            for tap in range(1, taps):
                total = total + weights[tap] * window[tap : tap + REACH, :]
            shifted.append(total)
        return (
            shifted[0] * cosine - shifted[1] * sine,
            shifted[0] * sine + shifted[1] * cosine,
        )

    def merge(level, step):
        def arrive(at):
            if level > 0:
                inter_copy(level, at).wait_recv()
            else:
                first_copy(at, 0).wait_recv()

                @pl.when(owner_of(at) != core)
                def _():
                    sibling_copy(at).wait_recv()

        if level > 0:

            @pl.when(step == 0)
            def _():
                arrive(0)

        @pl.when(step + 1 < steps)
        def _():
            arrive(step + 1)

        here = pl.ds(pl.multiple_of(step * REACH, REACH), REACH)
        for tile in range(tiles):
            terms = [term(level, slot, step, tile) for slot in range(2)]
            for part in range(2):
                total = terms[0][part] + terms[1][part]
                if level + 1 < levels:
                    columns = pl.ds(pl.multiple_of(first_row + tile * LANES, LANES), LANES)
                    image[level, part, here, columns] = total.astype(BF16)
                else:
                    merged[part, here, tile * LANES : (tile + 1) * LANES] = total
        if level + 1 < levels:
            merge_copy(level + 1, step, first_row).start()
        else:

            @pl.when(lax.rem(step, per_owner) == per_owner - 1)
            def _():
                owner = step // per_owner
                block = pl.ds(pl.multiple_of(owner * span, span), span)

                @pl.when(owner == core)
                def _():
                    for part in range(2):
                        out[0, part, pl.ds(first_row, share), :] = merged[part, block, :].T.astype(BF16)

                @pl.when(owner != core)
                def _():
                    for part in range(2):
                        handed[part] = merged[part, block, :].T.astype(BF16)
                    last_copy(first_row).start()

    first_copy(0, 0).wait_recv()

    @pl.when(core != 0)
    def _():
        sibling_copy(0).wait_recv()

        @pl.loop(0, per_owner)
        def _(j):
            for place in range(2):
                first_copy(core * per_owner + j, place).start()

    stages = [(merge, 0, MERGE_LAGS[0])]
    for level in range(1, levels):
        stages.append((send, level, SEND_LAGS[level]))
        stages.append((merge, level, MERGE_LAGS[level]))
    lag = MERGE_LAGS[levels - 1]

    @pl.loop(0, steps + lag)
    def _(tick):
        for stage, level, late in stages:

            @pl.when((tick >= late) & (tick < late + steps))
            def _():
                stage(level, tick - late)

    @pl.loop(0, steps)
    def _(step):
        for level in range(1, levels):
            inter_copy(level, step).wait_send()
            merge_copy(level, step, first_row).wait_send()

    @pl.loop(0, per_owner)
    def _(j):
        step = core * per_owner + j
        sibling_copy(step).wait_send()
        for place in range(2):
            first_copy(step, place).wait_send()

    last = last_copy(first_row)
    last.wait_send()
    last_copy(other_row).wait_recv()


def body(images, interp_matrix, offsets, tap_index, tap_table, phase_base, phase_slope):
    cores = lax.axis_size("range")
    levels = offsets.shape[0]
    angles = images.shape[2]
    span = images.shape[3]
    width = span * cores
    share = angles // cores
    steps = width // REACH
    vmem = pl.BlockSpec(memory_space=pltpu.VMEM)
    anywhere = pl.BlockSpec(memory_space=pl.ANY)
    framed = width + 2 * REACH
    return pl.pallas_call(
        functools.partial(kernel, levels),
        out_shape=pltpu.VMEM(images.shape, images.dtype),
        in_specs=[
            anywhere,
            anywhere,
            anywhere,
            anywhere,
            pl.BlockSpec(memory_space=pltpu.SMEM),
            anywhere,
            anywhere,
        ],
        out_specs=vmem,
        scratch_shapes=[
            pltpu.VMEM(images.shape[1:], images.dtype),
            pltpu.VMEM(offsets.shape, offsets.dtype),
            pltpu.VMEM(tap_index.shape, tap_index.dtype),
            pltpu.VMEM(phase_base.shape, F32),
            pltpu.VMEM(phase_slope.shape, F32),
            pltpu.VMEM((2, span, angles), BF16),
            pltpu.VMEM((levels - 1, 2, width, angles), BF16),
            pltpu.VMEM((2 * cores, share, angles), BF16),
            pltpu.VMEM((levels, 2, 16, share), F32),
            pltpu.VMEM((levels, 2, 2, width, share), F32),
            pltpu.VMEM((3, 2, span, share), BF16),
            pltpu.VMEM((levels - 1, 2, width, share), BF16),
            pltpu.VMEM((levels, 2, framed, share), BF16),
            pltpu.VMEM((levels, 2, framed, share), BF16),
            pltpu.VMEM((share // LANES, 2, 2, REACH + 2 * FINE, LANES), F32),
            pltpu.VMEM((2, width, share), F32),
            pltpu.VMEM((2, share, span), BF16),
            pltpu.SemaphoreType.DMA((6,)),
            pltpu.SemaphoreType.DMA((2, steps // cores)),
            pltpu.SemaphoreType.DMA((2, steps)),
            pltpu.SemaphoreType.DMA((2, levels, steps)),
            pltpu.SemaphoreType.DMA((2, levels - 1, steps)),
            pltpu.SemaphoreType.DMA((2,)),
        ],
        compiler_params=pltpu.CompilerParams(collective_id=0, has_side_effects=True),
    )(images, interp_matrix.reshape(2 * cores, share, angles), offsets, tap_index, tap_table.T, phase_base, phase_slope)


def solution(mesh):
    return jax.shard_map(
        body,
        mesh=mesh,
        in_specs=(P(("scene", "aper"), None, None, "range"), P(), P(), P(), P(), P(), P()),
        out_specs=P(("scene", "aper"), None, None, "range"),
        check_vma=False,
    )
```

```python
import functools

import jax
import jax.numpy as jnp
from jax import lax
from jax.experimental import pallas as pl
from jax.experimental.pallas import tpu as pltpu
from jax.sharding import PartitionSpec as P

MESH = pl.DeviceIdType.MESH
LANES = 128
REACH = 32
FINE = 8
EARLY = 2
LEADS = (0, 0, 0)
COUNTS = (0, 1, 1)
SEND_LAGS = (0, 1, 7)
MERGE_LAGS = (0, 6, 16)
F32 = jnp.float32
BF16 = jnp.bfloat16


def sincos(angle):
    turns = jnp.floor(angle * 0.6366197723675814 + 0.5)
    rest = angle - turns * 1.5703125
    rest = rest - turns * 4.837512969970703125e-4
    rest = rest - turns * 7.54978995489188216e-8
    quadrant = turns.astype(jnp.int32)
    square = rest * rest
    sine = rest + rest * square * (
        -1.6666654611e-1 + square * (8.3321608736e-3 + square * -1.9515295891e-4)
    )
    cosine = (1.0 - 0.5 * square) + square * square * (
        4.166664568298827e-2 + square * (-1.388731625493765e-3 + square * 2.443315711809948e-5)
    )
    odd = (quadrant & 1) == 1
    swapped_sine = jnp.where(odd, cosine, sine)
    swapped_cosine = jnp.where(odd, sine, cosine)
    sine = jnp.where((quadrant & 2) == 2, -swapped_sine, swapped_sine)
    cosine = jnp.where(((quadrant + 1) & 2) == 2, -swapped_cosine, swapped_cosine)
    return sine, cosine


def kernel(
    levels,
    images_in,
    matrix,
    offsets_in,
    tap_index_in,
    tap_table_in,
    phase_base_in,
    phase_slope_in,
    out,
    images,
    offsets,
    tap_index,
    tap_table,
    phase_base,
    phase_slope,
    source,
    image,
    rows_of,
    params,
    trig,
    staging,
    outgoing,
    incoming,
    kept,
    windows,
    handed,
    assembled,
    local_sem,
    sent_sem,
    sibling_sem,
    inter_sem,
    merge_sem,
    last_sem,
):
    width = image.shape[2]
    angles = image.shape[3]
    span = images.shape[2]
    share = rows_of.shape[1]
    cores = angles // share
    tiles = share // LANES
    steps = width // REACH
    per_owner = span // REACH
    taps = tap_table.shape[0]
    scene = lax.axis_index("scene")
    aper = lax.axis_index("aper")
    core = lax.axis_index("range")
    other = 1 - core
    first_row = pl.multiple_of(core * share, share)
    other_row = pl.multiple_of(other * share, share)
    halves = [lax.rem(aper // 2**level, 2) for level in range(levels)]
    partners = [aper + (1 - 2 * halves[level]) * 2**level for level in range(levels)]

    barrier = pltpu.get_barrier_semaphore()
    for partner in partners:
        pl.semaphore_signal(barrier, inc=1, device_id=(scene, partner, core), device_id_type=MESH)
    pl.semaphore_signal(barrier, inc=1, device_id=(scene, aper, other), device_id_type=MESH)

    pl.semaphore_signal(
        barrier, inc=1, device_id=(scene, partners[0], other), device_id_type=MESH
    )

    local_copies = [
        pltpu.make_async_copy(images_in.at[0], images, local_sem.at[0]),
        pltpu.make_async_copy(matrix, rows_of, local_sem.at[1]),
        pltpu.make_async_copy(offsets_in, offsets, local_sem.at[2]),
        pltpu.make_async_copy(tap_index_in, tap_index, local_sem.at[3]),
        pltpu.make_async_copy(phase_base_in, phase_base, local_sem.at[4]),
        pltpu.make_async_copy(phase_slope_in, phase_slope, local_sem.at[5]),
        pltpu.make_async_copy(tap_table_in, tap_table, local_sem.at[6]),
    ]
    for copy in local_copies:
        copy.start()

    def frame(step):
        return pl.ds(pl.multiple_of((step + 1) * REACH, REACH), REACH)

    def plain(step):
        return pl.ds(pl.multiple_of(step * REACH, REACH), REACH)

    def owner_of(step):
        return step // per_owner

    def local_step(step):
        return lax.rem(step, per_owner)

    def sibling_copy(step):
        return pltpu.make_async_remote_copy(
            src_ref=staging.at[0, :, plain(local_step(step)), :],
            dst_ref=kept.at[0, :, frame(step), :],
            send_sem=sent_sem.at[2 * levels],
            recv_sem=sibling_sem.at[step],
            device_id=(scene, aper, other),
            device_id_type=MESH,
        )

    def first_copy(step, place):
        return pltpu.make_async_remote_copy(
            src_ref=staging.at[1 + place, :, plain(local_step(step)), :],
            dst_ref=incoming.at[0, :, frame(step), :],
            send_sem=sent_sem.at[0],
            recv_sem=inter_sem.at[0, step],
            device_id=(scene, partners[0], core if place == 0 else other),
            device_id_type=MESH,
        )

    def inter_copy(level, step):
        return pltpu.make_async_remote_copy(
            src_ref=outgoing.at[level - 1, :, plain(step), :],
            dst_ref=incoming.at[level, :, frame(step), :],
            send_sem=sent_sem.at[level],
            recv_sem=inter_sem.at[level, step],
            device_id=(scene, partners[level], core),
            device_id_type=MESH,
        )

    def product(both, row):
        return lax.dot_general(
            both, row, (((1,), (1,)), ((), ())), preferred_element_type=F32
        ).astype(BF16)

    def first_products(j):
        step = core * per_owner + j
        both = jnp.concatenate([source[part, plain(j), :] for part in range(2)], axis=0)
        mine = halves[0] * cores
        yours = (1 - halves[0]) * cores
        for place, block in enumerate((mine + other, yours + core, yours + other)):
            inter = product(both, rows_of[block])
            for part in range(2):
                staging[place, part, plain(j), :] = inter[part * REACH : (part + 1) * REACH]
        inter = product(both, rows_of[mine + core])
        for part in range(2):
            kept[0, part, frame(step), :] = inter[part * REACH : (part + 1) * REACH]

    local_copies[0].wait()
    for part in range(2):
        source[part] = images[part].T
    local_copies[1].wait()
    for j in range(EARLY):
        first_products(j)
    edge = jnp.zeros((2, REACH, share), BF16)
    for level in range(levels):
        for buffer in (incoming, kept):
            buffer[level, :, 0:REACH, :] = edge
            buffer[level, :, REACH + width : REACH + width + REACH, :] = edge

    pl.semaphore_wait(barrier, len(partners) + 2)

    @pl.loop(0, per_owner)
    def _(j):
        step = core * per_owner + j

        @pl.when(j >= EARLY)
        def _():
            first_products(j)

        sibling_copy(step).start()

        @pl.when(core == 0)
        def _():
            for place in range(2):
                first_copy(step, place).start()

    for copy in local_copies[2:]:
        copy.wait()

    def tables(level):
        half = halves[level]
        picked = pl.ds(pl.multiple_of(half * angles + core * share, LANES), share)
        index = tap_index[level, :, picked]
        weights = [jnp.zeros(index.shape, F32) for _ in range(taps)]
        for entry in range(tap_table.shape[1]):
            hit = index == entry
            for tap in range(taps):
                weights[tap] = jnp.where(hit, tap_table[tap, entry], weights[tap])
        base = phase_base[level, :, picked]
        slope = phase_slope[level, :, picked]
        lines = weights + [offsets[level, :, picked].astype(F32) + float(REACH - 3), base, slope]
        for row, line in enumerate(lines):
            for slot in range(2):
                role = half if slot == 0 else 1 - half
                params[level, slot, row : row + 1, :] = jnp.where(role == 0, line[0:1], line[1:2])
        for slot in range(2):
            for tile in range(tiles):
                columns = slice(tile * LANES, (tile + 1) * LANES)

                def line(row, count):
                    return jnp.broadcast_to(
                        params[level, slot, row : row + 1, columns], (count, LANES)
                    )

                fine = lax.broadcasted_iota(jnp.int32, (REACH, LANES), 0).astype(F32)
                coarse = (
                    lax.broadcasted_iota(jnp.int32, (steps, LANES), 0) * REACH
                ).astype(F32)
                near = sincos(line(taps + 2, REACH) * fine)
                far = sincos(line(taps + 1, steps) + line(taps + 2, steps) * coarse)
                for step in range(steps):
                    sine = jnp.broadcast_to(far[0][step : step + 1], (REACH, LANES))
                    cosine = jnp.broadcast_to(far[1][step : step + 1], (REACH, LANES))
                    place = pl.ds(step * REACH, REACH)
                    trig[level, slot, 0, place, columns] = sine * near[1] + cosine * near[0]
                    trig[level, slot, 1, place, columns] = cosine * near[1] - sine * near[0]

    for level in range(levels):
        tables(level)

    def merge_copy(level, step, row):
        place = image.at[
            level - 1, :, pl.ds(pl.multiple_of(step * REACH, REACH), REACH), pl.ds(row, share)
        ]
        return pltpu.make_async_remote_copy(
            src_ref=place,
            dst_ref=place,
            send_sem=sent_sem.at[levels + level - 1],
            recv_sem=merge_sem.at[level - 1, step],
            device_id=(scene, aper, other),
            device_id_type=MESH,
        )

    def last_copy(step, row):
        return pltpu.make_async_remote_copy(
            src_ref=handed.at[:, plain(step), :],
            dst_ref=assembled.at[:, plain(local_step(step)), pl.ds(row, share)],
            send_sem=sent_sem.at[2 * levels - 1],
            recv_sem=last_sem.at[step],
            device_id=(scene, aper, other),
            device_id_type=MESH,
        )

    def send(level, step):
        merge_copy(level, step, other_row).wait_recv()
        here = plain(step)
        both = jnp.concatenate([image[level - 1, part, here, :] for part in range(2)], axis=0)
        away = product(both, rows_of[(1 - halves[level]) * cores + core])
        home = product(both, rows_of[halves[level] * cores + core])
        for part in range(2):
            outgoing[level - 1, part, here, :] = away[part * REACH : (part + 1) * REACH]
            kept[level, part, frame(step), :] = home[part * REACH : (part + 1) * REACH]
        inter_copy(level, step).start()

    def term(level, slot, step, tile):
        buffer = kept if slot == 0 else incoming
        columns = slice(tile * LANES, (tile + 1) * LANES)

        def line(row, count):
            return jnp.broadcast_to(params[level, slot, row : row + 1, columns], (count, LANES))

        amount = line(taps, 2 * REACH).astype(jnp.int32)
        weights = [line(tap, REACH) for tap in range(taps)]
        sine, cosine = [trig[level, slot, which, plain(step), columns] for which in range(2)]
        shifted = []
        for part in range(2):
            value = buffer[
                level, part, pl.ds(pl.multiple_of(step * REACH, REACH), 3 * REACH), columns
            ].astype(F32)
            keep = 2 * REACH
            bit = REACH
            value = jnp.concatenate(
                [
                    jnp.where((amount & bit) == bit, value[bit:], value[:keep]),
                    value[keep : keep + FINE],
                ],
                axis=0,
            )
            while bit > FINE:
                bit //= 2
                keep = value.shape[0] - bit
                value = jnp.where((amount[:keep] & bit) == bit, value[bit:], value[:keep])
            while bit > 1:
                bit //= 2
                turned = pltpu.roll(value, value.shape[0] - bit, 0)
                value = jnp.where((amount[: value.shape[0]] & bit) == bit, turned, value)
            window = windows.at[tile, slot, part]
            window[...] = value
            total = weights[0] * value[:REACH]
            for tap in range(1, taps):
                total = total + weights[tap] * window[tap : tap + REACH, :]
            shifted.append(total)
        return (
            shifted[0] * cosine - shifted[1] * sine,
            shifted[0] * sine + shifted[1] * cosine,
        )

    def merge(level, step):
        def arrive(at):
            if level > 0:
                inter_copy(level, at).wait_recv()
            else:
                first_copy(at, 0).wait_recv()

                @pl.when(owner_of(at) != core)
                def _():
                    sibling_copy(at).wait_recv()

        if level > 0:

            @pl.when(step == 0)
            def _():
                arrive(0)

        @pl.when(step + 1 < steps)
        def _():
            arrive(step + 1)

        here = pl.ds(pl.multiple_of(step * REACH, REACH), REACH)
        for tile in range(tiles):
            terms = [term(level, slot, step, tile) for slot in range(2)]
            for part in range(2):
                total = terms[0][part] + terms[1][part]
                if level + 1 < levels:
                    columns = pl.ds(pl.multiple_of(first_row + tile * LANES, LANES), LANES)
                    image[level, part, here, columns] = total.astype(BF16)
                else:
                    value = total.astype(BF16)

                    @pl.when(owner_of(step) == core)
                    def _():
                        columns = pl.ds(pl.multiple_of(first_row + tile * LANES, LANES), LANES)
                        assembled[part, plain(local_step(step)), columns] = value

                    @pl.when(owner_of(step) != core)
                    def _():
                        handed[part, here, tile * LANES : (tile + 1) * LANES] = value
        if level + 1 < levels:
            merge_copy(level + 1, step, first_row).start()
        else:

            @pl.when(owner_of(step) != core)
            def _():
                last_copy(step, first_row).start()

    first_copy(0, 0).wait_recv()

    @pl.when(core != 0)
    def _():
        sibling_copy(0).wait_recv()

        @pl.loop(0, per_owner)
        def _(j):
            for place in range(2):
                first_copy(core * per_owner + j, place).start()

    stages = [(merge, 0, MERGE_LAGS[0])]
    for level in range(1, levels):
        stages.append((send, level, SEND_LAGS[level]))
        stages.append((merge, level, MERGE_LAGS[level]))
    lag = MERGE_LAGS[levels - 1]

    @pl.loop(0, steps + lag)
    def _(tick):
        for stage, level, late in stages:

            lead = LEADS[level] if stage is send else 0

            @pl.when((tick >= late - lead) & (tick < late + steps))
            def _():
                if stage is send:
                    count = COUNTS[level]
                    first = tick == late - LEADS[level]
                    low = jnp.where(first, 0, jnp.maximum(count, tick - late))
                    high = jnp.where(first, count, tick - late + 1)

                    @pl.loop(low, high)
                    def _(step):
                        send(level, step)

                else:
                    stage(level, tick - late)

    @pl.loop(0, per_owner)
    def _(j):
        last_copy(core * per_owner + j, other_row).wait_recv()

    for part in range(2):
        out[0, part] = assembled[part].T

    def all_sent(ref, sem):
        pltpu.make_async_remote_copy(
            src_ref=ref,
            dst_ref=ref,
            send_sem=sent_sem.at[sem],
            recv_sem=last_sem.at[0],
            device_id=(scene, aper, other),
            device_id_type=MESH,
        ).wait_send()

    all_sent(staging.at[0], 2 * levels)
    all_sent(staging.at[pl.ds(1, 2)], 0)
    for level in range(1, levels):
        all_sent(outgoing.at[level - 1], level)
        all_sent(image.at[level - 1, :, :, pl.ds(first_row, share)], levels + level - 1)
    theirs = pl.ds(pl.multiple_of(other * span, span), span)
    all_sent(handed.at[:, theirs, :], 2 * levels - 1)


def body(images, interp_matrix, offsets, tap_index, tap_table, phase_base, phase_slope):
    cores = lax.axis_size("range")
    levels = offsets.shape[0]
    angles = images.shape[2]
    span = images.shape[3]
    width = span * cores
    share = angles // cores
    steps = width // REACH
    vmem = pl.BlockSpec(memory_space=pltpu.VMEM)
    anywhere = pl.BlockSpec(memory_space=pl.ANY)
    framed = width + 2 * REACH
    return pl.pallas_call(
        functools.partial(kernel, levels),
        out_shape=pltpu.VMEM(images.shape, images.dtype),
        in_specs=[
            anywhere,
            anywhere,
            anywhere,
            anywhere,
            anywhere,
            anywhere,
            anywhere,
        ],
        out_specs=vmem,
        scratch_shapes=[
            pltpu.VMEM(images.shape[1:], images.dtype),
            pltpu.VMEM(offsets.shape, offsets.dtype),
            pltpu.VMEM(tap_index.shape, tap_index.dtype),
            pltpu.SMEM(tap_table.shape[::-1], F32),
            pltpu.VMEM(phase_base.shape, F32),
            pltpu.VMEM(phase_slope.shape, F32),
            pltpu.VMEM((2, span, angles), BF16),
            pltpu.VMEM((levels - 1, 2, width, angles), BF16),
            pltpu.VMEM((2 * cores, share, angles), BF16),
            pltpu.VMEM((levels, 2, 16, share), F32),
            pltpu.VMEM((levels, 2, 2, width, share), F32),
            pltpu.VMEM((3, 2, span, share), BF16),
            pltpu.VMEM((levels - 1, 2, width, share), BF16),
            pltpu.VMEM((levels, 2, framed, share), BF16),
            pltpu.VMEM((levels, 2, framed, share), BF16),
            pltpu.VMEM((share // LANES, 2, 2, REACH + 2 * FINE, LANES), F32),
            pltpu.VMEM((2, width, share), BF16),
            pltpu.VMEM((2, span, angles), BF16),
            pltpu.SemaphoreType.DMA((7,)),
            pltpu.SemaphoreType.DMA((2 * levels + 1,)),
            pltpu.SemaphoreType.DMA((steps,)),
            pltpu.SemaphoreType.DMA((levels, steps)),
            pltpu.SemaphoreType.DMA((levels - 1, steps)),
            pltpu.SemaphoreType.DMA((steps,)),
        ],
        compiler_params=pltpu.CompilerParams(collective_id=0, has_side_effects=True),
    )(images, interp_matrix.reshape(2 * cores, share, angles), offsets, tap_index, tap_table.T, phase_base, phase_slope)


def solution(mesh):
    return jax.shard_map(
        body,
        mesh=mesh,
        in_specs=(P(("scene", "aper"), None, None, "range"), P(), P(), P(), P(), P(), P()),
        out_specs=P(("scene", "aper"), None, None, "range"),
        check_vma=False,
    )
```

```python
import functools

import jax
import jax.numpy as jnp
from jax import lax
from jax.experimental import pallas as pl
from jax.experimental.pallas import tpu as pltpu
from jax.sharding import PartitionSpec as P

MESH = pl.DeviceIdType.MESH
LANES = 128
REACH = 32
FINE = 8
EARLY = 1
LEADS = (0, 0, 0)
COUNTS = (0, 1, 0)
PAIRED = ((False, True), (True, False), (False, False))
SEND_FIRST = True
WAIT_FIRST = True
SEND_LAGS = (0, 1, 7)
MERGE_LAGS = (0, 6, 16)
F32 = jnp.float32
BF16 = jnp.bfloat16


def sincos(angle):
    turns = jnp.floor(angle * 0.6366197723675814 + 0.5)
    rest = angle - turns * 1.5703125
    rest = rest - turns * 4.837512969970703125e-4
    rest = rest - turns * 7.54978995489188216e-8
    quadrant = turns.astype(jnp.int32)
    square = rest * rest
    sine = rest + rest * square * (
        -1.6666654611e-1 + square * (8.3321608736e-3 + square * -1.9515295891e-4)
    )
    cosine = (1.0 - 0.5 * square) + square * square * (
        4.166664568298827e-2 + square * (-1.388731625493765e-3 + square * 2.443315711809948e-5)
    )
    odd = (quadrant & 1) == 1
    swapped_sine = jnp.where(odd, cosine, sine)
    swapped_cosine = jnp.where(odd, sine, cosine)
    sine = jnp.where((quadrant & 2) == 2, -swapped_sine, swapped_sine)
    cosine = jnp.where(((quadrant + 1) & 2) == 2, -swapped_cosine, swapped_cosine)
    return sine, cosine


def kernel(
    levels,
    images_in,
    matrix,
    offsets_in,
    tap_index_in,
    tap_table_in,
    phase_base_in,
    phase_slope_in,
    out,
    images,
    offsets,
    tap_index,
    tap_table,
    phase_base,
    phase_slope,
    source,
    image,
    rows_of,
    params,
    trig,
    staging,
    outgoing,
    incoming,
    kept,
    windows,
    handed,
    assembled,
    local_sem,
    sent_sem,
    sibling_sem,
    inter_sem,
    merge_sem,
    last_sem,
):
    width = image.shape[2]
    angles = image.shape[3]
    span = images.shape[2]
    share = rows_of.shape[1]
    cores = angles // share
    tiles = share // LANES
    steps = width // REACH
    per_owner = span // REACH
    taps = tap_table.shape[0]
    scene = lax.axis_index("scene")
    aper = lax.axis_index("aper")
    core = lax.axis_index("range")
    other = 1 - core
    first_row = pl.multiple_of(core * share, share)
    other_row = pl.multiple_of(other * share, share)
    halves = [lax.rem(aper // 2**level, 2) for level in range(levels)]
    partners = [aper + (1 - 2 * halves[level]) * 2**level for level in range(levels)]

    barrier = pltpu.get_barrier_semaphore()
    for partner in partners:
        pl.semaphore_signal(barrier, inc=1, device_id=(scene, partner, core), device_id_type=MESH)
    pl.semaphore_signal(barrier, inc=1, device_id=(scene, aper, other), device_id_type=MESH)

    pl.semaphore_signal(
        barrier, inc=1, device_id=(scene, partners[0], other), device_id_type=MESH
    )

    local_copies = [
        pltpu.make_async_copy(images_in.at[0], images, local_sem.at[0]),
        pltpu.make_async_copy(matrix, rows_of, local_sem.at[1]),
        pltpu.make_async_copy(offsets_in, offsets, local_sem.at[2]),
        pltpu.make_async_copy(tap_index_in, tap_index, local_sem.at[3]),
        pltpu.make_async_copy(phase_base_in, phase_base, local_sem.at[4]),
        pltpu.make_async_copy(phase_slope_in, phase_slope, local_sem.at[5]),
        pltpu.make_async_copy(tap_table_in, tap_table, local_sem.at[6]),
    ]
    for copy in local_copies:
        copy.start()

    def frame(step):
        return pl.ds(pl.multiple_of((step + 1) * REACH, REACH), REACH)

    def plain(step):
        return pl.ds(pl.multiple_of(step * REACH, REACH), REACH)

    def owner_of(step):
        return step // per_owner

    def local_step(step):
        return lax.rem(step, per_owner)

    def sibling_copy(step):
        return pltpu.make_async_remote_copy(
            src_ref=staging.at[0, :, plain(local_step(step)), :],
            dst_ref=kept.at[0, :, frame(step), :],
            send_sem=sent_sem.at[2 * levels],
            recv_sem=sibling_sem.at[step],
            device_id=(scene, aper, other),
            device_id_type=MESH,
        )

    def first_copy(step, place):
        return pltpu.make_async_remote_copy(
            src_ref=staging.at[1 + place, :, plain(local_step(step)), :],
            dst_ref=incoming.at[0, :, frame(step), :],
            send_sem=sent_sem.at[0],
            recv_sem=inter_sem.at[0, step],
            device_id=(scene, partners[0], core if place == 0 else other),
            device_id_type=MESH,
        )

    def inter_copy(level, step):
        return pltpu.make_async_remote_copy(
            src_ref=outgoing.at[level - 1, :, plain(step), :],
            dst_ref=incoming.at[level, :, frame(step), :],
            send_sem=sent_sem.at[level],
            recv_sem=inter_sem.at[level, step],
            device_id=(scene, partners[level], core),
            device_id_type=MESH,
        )

    def product(both, row):
        return lax.dot_general(
            both, row, (((1,), (1,)), ((), ())), preferred_element_type=F32
        ).astype(BF16)

    def first_products(j):
        step = core * per_owner + j
        both = jnp.concatenate([source[part, plain(j), :] for part in range(2)], axis=0)
        mine = halves[0] * cores
        yours = (1 - halves[0]) * cores
        for place, block in enumerate((mine + other, yours + core, yours + other)):
            inter = product(both, rows_of[block])
            for part in range(2):
                staging[place, part, plain(j), :] = inter[part * REACH : (part + 1) * REACH]
        inter = product(both, rows_of[mine + core])
        for part in range(2):
            kept[0, part, frame(step), :] = inter[part * REACH : (part + 1) * REACH]

    local_copies[0].wait()
    for part in range(2):
        source[part] = images[part].T
    local_copies[1].wait()
    for j in range(EARLY):
        first_products(j)
    edge = jnp.zeros((2, REACH, share), BF16)
    for level in range(levels):
        for buffer in (incoming, kept):
            buffer[level, :, 0:REACH, :] = edge
            buffer[level, :, REACH + width : REACH + width + REACH, :] = edge

    pl.semaphore_wait(barrier, len(partners) + 2)

    @pl.loop(0, per_owner)
    def _(j):
        step = core * per_owner + j

        @pl.when(j >= EARLY)
        def _():
            first_products(j)

        sibling_copy(step).start()

        @pl.when(core == 0)
        def _():
            for place in range(2):
                first_copy(step, place).start()

    for copy in local_copies[2:]:
        copy.wait()

    def tables(level):
        half = halves[level]
        picked = pl.ds(pl.multiple_of(half * angles + core * share, LANES), share)
        index = tap_index[level, :, picked]
        weights = [jnp.zeros(index.shape, F32) for _ in range(taps)]
        for entry in range(tap_table.shape[1]):
            hit = index == entry
            for tap in range(taps):
                weights[tap] = jnp.where(hit, tap_table[tap, entry], weights[tap])
        base = phase_base[level, :, picked]
        slope = phase_slope[level, :, picked]
        lines = weights + [offsets[level, :, picked].astype(F32) + float(REACH - 3), base, slope]
        for row, line in enumerate(lines):
            for slot in range(2):
                role = half if slot == 0 else 1 - half
                params[level, slot, row : row + 1, :] = jnp.where(role == 0, line[0:1], line[1:2])
        for slot in range(2):
            for tile in range(tiles):
                columns = slice(tile * LANES, (tile + 1) * LANES)

                def line(row, count):
                    return jnp.broadcast_to(
                        params[level, slot, row : row + 1, columns], (count, LANES)
                    )

                fine = lax.broadcasted_iota(jnp.int32, (REACH, LANES), 0).astype(F32)
                coarse = (
                    lax.broadcasted_iota(jnp.int32, (steps, LANES), 0) * REACH
                ).astype(F32)
                near = sincos(line(taps + 2, REACH) * fine)
                far = sincos(line(taps + 1, steps) + line(taps + 2, steps) * coarse)
                for step in range(steps):
                    sine = jnp.broadcast_to(far[0][step : step + 1], (REACH, LANES))
                    cosine = jnp.broadcast_to(far[1][step : step + 1], (REACH, LANES))
                    place = pl.ds(step * REACH, REACH)
                    trig[level, slot, 0, place, columns] = sine * near[1] + cosine * near[0]
                    trig[level, slot, 1, place, columns] = cosine * near[1] - sine * near[0]

    for level in range(levels):
        tables(level)

    def merge_copy(level, step, row):
        place = image.at[
            level - 1, :, pl.ds(pl.multiple_of(step * REACH, REACH), REACH), pl.ds(row, share)
        ]
        return pltpu.make_async_remote_copy(
            src_ref=place,
            dst_ref=place,
            send_sem=sent_sem.at[levels + level - 1],
            recv_sem=merge_sem.at[level - 1, step],
            device_id=(scene, aper, other),
            device_id_type=MESH,
        )

    def last_copy(step, row):
        return pltpu.make_async_remote_copy(
            src_ref=handed.at[:, plain(step), :],
            dst_ref=assembled.at[:, plain(local_step(step)), pl.ds(row, share)],
            send_sem=sent_sem.at[2 * levels - 1],
            recv_sem=last_sem.at[step],
            device_id=(scene, aper, other),
            device_id_type=MESH,
        )

    def send(level, step):
        merge_copy(level, step, other_row).wait_recv()
        here = plain(step)
        both = jnp.concatenate([image[level - 1, part, here, :] for part in range(2)], axis=0)
        away = product(both, rows_of[(1 - halves[level]) * cores + core])
        home = product(both, rows_of[halves[level] * cores + core])
        for part in range(2):
            outgoing[level - 1, part, here, :] = away[part * REACH : (part + 1) * REACH]
            kept[level, part, frame(step), :] = home[part * REACH : (part + 1) * REACH]
        inter_copy(level, step).start()

    def term(level, slot, step, tile):
        buffer = kept if slot == 0 else incoming
        columns = slice(tile * LANES, (tile + 1) * LANES)

        def line(row, count):
            return jnp.broadcast_to(params[level, slot, row : row + 1, columns], (count, LANES))

        amount = line(taps, 2 * REACH).astype(jnp.int32)
        weights = [line(tap, REACH) for tap in range(taps)]
        sine, cosine = [trig[level, slot, which, plain(step), columns] for which in range(2)]
        shifted = []
        for part in range(2):
            value = buffer[
                level, part, pl.ds(pl.multiple_of(step * REACH, REACH), 3 * REACH), columns
            ].astype(F32)
            keep = 2 * REACH
            bit = REACH
            value = jnp.concatenate(
                [
                    jnp.where((amount & bit) == bit, value[bit:], value[:keep]),
                    value[keep : keep + FINE],
                ],
                axis=0,
            )
            while bit > FINE:
                bit //= 2
                keep = value.shape[0] - bit
                value = jnp.where((amount[:keep] & bit) == bit, value[bit:], value[:keep])
            while bit > 1:
                bit //= 2
                turned = pltpu.roll(value, value.shape[0] - bit, 0)
                value = jnp.where((amount[: value.shape[0]] & bit) == bit, turned, value)
            window = windows.at[tile, slot, part]
            window[...] = value
            total = weights[0] * value[:REACH]
            for tap in range(1, taps):
                total = total + weights[tap] * window[tap : tap + REACH, :]
            shifted.append(total)
        return (
            shifted[0] * cosine - shifted[1] * sine,
            shifted[0] * sine + shifted[1] * cosine,
        )

    def merge(level, step):
        def arrive(at):
            if level > 0:
                inter_copy(level, at).wait_recv()
            else:
                first_copy(at, 0).wait_recv()

                @pl.when(owner_of(at) != core)
                def _():
                    sibling_copy(at).wait_recv()

        if level > 0:

            @pl.when(step == 0)
            def _():
                arrive(0)

        @pl.when(step + 1 < steps)
        def _():
            arrive(step + 1)

        here = pl.ds(pl.multiple_of(step * REACH, REACH), REACH)
        for tile in range(tiles):
            terms = [term(level, slot, step, tile) for slot in range(2)]
            for part in range(2):
                total = terms[0][part] + terms[1][part]
                if level + 1 < levels:
                    columns = pl.ds(pl.multiple_of(first_row + tile * LANES, LANES), LANES)
                    image[level, part, here, columns] = total.astype(BF16)
                else:
                    value = total.astype(BF16)

                    @pl.when(owner_of(step) == core)
                    def _():
                        columns = pl.ds(pl.multiple_of(first_row + tile * LANES, LANES), LANES)
                        assembled[part, plain(local_step(step)), columns] = value

                    @pl.when(owner_of(step) != core)
                    def _():
                        handed[part, here, tile * LANES : (tile + 1) * LANES] = value
        if level + 1 < levels:
            merge_copy(level + 1, step, first_row).start()
        else:

            @pl.when(owner_of(step) != core)
            def _():
                last_copy(step, first_row).start()

    if WAIT_FIRST:
        first_copy(0, 0).wait_recv()

    @pl.when(core != 0)
    def _():
        @pl.loop(0, per_owner)
        def _(j):
            for place in range(2):
                first_copy(core * per_owner + j, place).start()

        sibling_copy(0).wait_recv()

    if not WAIT_FIRST:
        first_copy(0, 0).wait_recv()

    stages = [(merge, 0, MERGE_LAGS[0])]
    for level in range(1, levels):
        stages.append((send, level, SEND_LAGS[level]))
        if level > 1:
            stages.append((merge, level - 1, MERGE_LAGS[level - 1]))
    if SEND_FIRST:
        stages = [(merge, 0, MERGE_LAGS[0])]
        stages += [(send, level, SEND_LAGS[level]) for level in range(1, levels)]
        stages += [(merge, level, MERGE_LAGS[level]) for level in range(1, levels - 1)]
    stages.append((merge, levels - 1, MERGE_LAGS[levels - 1]))
    lag = MERGE_LAGS[levels - 1]

    @pl.loop(0, steps + lag)
    def _(tick):
        for stage, level, late in stages:
            sends = stage is send
            lead = LEADS[level] if sends else 0
            paired = PAIRED[level][0 if sends else 1]

            @pl.when((tick >= late - lead) & (tick < late + steps))
            def _():
                count = COUNTS[level] if sends else 0
                first = tick == late - lead
                low = jnp.maximum(count, tick - late)
                high = tick - late + 1
                if count:
                    low = jnp.where(first, 0, low)
                    high = jnp.where(first, count, high)
                if paired:
                    low = jnp.where(tick - late == steps - 1, steps, low)
                    high = jnp.where(tick - late == steps - 2, steps, high)
                if count or paired:

                    @pl.loop(low, high)
                    def _(step):
                        stage(level, step)

                else:
                    stage(level, tick - late)

    @pl.loop(0, per_owner)
    def _(j):
        last_copy(core * per_owner + j, other_row).wait_recv()

    for part in range(2):
        out[0, part] = assembled[part].T

    def all_sent(ref, sem):
        pltpu.make_async_remote_copy(
            src_ref=ref,
            dst_ref=ref,
            send_sem=sent_sem.at[sem],
            recv_sem=last_sem.at[0],
            device_id=(scene, aper, other),
            device_id_type=MESH,
        ).wait_send()

    all_sent(staging.at[0], 2 * levels)
    all_sent(staging.at[pl.ds(1, 2)], 0)
    for level in range(1, levels):
        all_sent(outgoing.at[level - 1], level)
        all_sent(image.at[level - 1, :, :, pl.ds(first_row, share)], levels + level - 1)
    theirs = pl.ds(pl.multiple_of(other * span, span), span)
    all_sent(handed.at[:, theirs, :], 2 * levels - 1)


def body(images, interp_matrix, offsets, tap_index, tap_table, phase_base, phase_slope):
    cores = lax.axis_size("range")
    levels = offsets.shape[0]
    angles = images.shape[2]
    span = images.shape[3]
    width = span * cores
    share = angles // cores
    steps = width // REACH
    vmem = pl.BlockSpec(memory_space=pltpu.VMEM)
    anywhere = pl.BlockSpec(memory_space=pl.ANY)
    framed = width + 2 * REACH
    return pl.pallas_call(
        functools.partial(kernel, levels),
        out_shape=pltpu.VMEM(images.shape, images.dtype),
        in_specs=[
            anywhere,
            anywhere,
            anywhere,
            anywhere,
            anywhere,
            anywhere,
            anywhere,
        ],
        out_specs=vmem,
        scratch_shapes=[
            pltpu.VMEM(images.shape[1:], images.dtype),
            pltpu.VMEM(offsets.shape, offsets.dtype),
            pltpu.VMEM(tap_index.shape, tap_index.dtype),
            pltpu.SMEM(tap_table.shape[::-1], F32),
            pltpu.VMEM(phase_base.shape, F32),
            pltpu.VMEM(phase_slope.shape, F32),
            pltpu.VMEM((2, span, angles), BF16),
            pltpu.VMEM((levels - 1, 2, width, angles), BF16),
            pltpu.VMEM((2 * cores, share, angles), BF16),
            pltpu.VMEM((levels, 2, 16, share), F32),
            pltpu.VMEM((levels, 2, 2, width, share), F32),
            pltpu.VMEM((3, 2, span, share), BF16),
            pltpu.VMEM((levels - 1, 2, width, share), BF16),
            pltpu.VMEM((levels, 2, framed, share), BF16),
            pltpu.VMEM((levels, 2, framed, share), BF16),
            pltpu.VMEM((share // LANES, 2, 2, REACH + 2 * FINE, LANES), F32),
            pltpu.VMEM((2, width, share), BF16),
            pltpu.VMEM((2, span, angles), BF16),
            pltpu.SemaphoreType.DMA((7,)),
            pltpu.SemaphoreType.DMA((2 * levels + 1,)),
            pltpu.SemaphoreType.DMA((steps,)),
            pltpu.SemaphoreType.DMA((levels, steps)),
            pltpu.SemaphoreType.DMA((levels - 1, steps)),
            pltpu.SemaphoreType.DMA((steps,)),
        ],
        compiler_params=pltpu.CompilerParams(collective_id=0, has_side_effects=True),
    )(images, interp_matrix.reshape(2 * cores, share, angles), offsets, tap_index, tap_table.T, phase_base, phase_slope)


def solution(mesh):
    return jax.shard_map(
        body,
        mesh=mesh,
        in_specs=(P(("scene", "aper"), None, None, "range"), P(), P(), P(), P(), P(), P()),
        out_specs=P(("scene", "aper"), None, None, "range"),
        check_vma=False,
    )
```

```python
import functools

import jax
import jax.numpy as jnp
from jax import lax
from jax.experimental import pallas as pl
from jax.experimental.pallas import tpu as pltpu
from jax.sharding import PartitionSpec as P

MESH = pl.DeviceIdType.MESH
LANES = 128
REACH = 32
FINE = 8
EARLY = 1
LEADS = (0, 0, 0)
COUNTS = (0, 1, 0)
PAIRED = ((False, True), (True, False), (False, False))
SEND_FIRST = True
WAIT_FIRST = True
SEND_LAGS = (0, 1, 7)
MERGE_LAGS = (0, 6, 16)
F32 = jnp.float32
BF16 = jnp.bfloat16


def sincos(angle):
    turns = jnp.floor(angle * 0.6366197723675814 + 0.5)
    rest = angle - turns * 1.5703125
    rest = rest - turns * 4.837512969970703125e-4
    rest = rest - turns * 7.54978995489188216e-8
    quadrant = turns.astype(jnp.int32)
    square = rest * rest
    sine = rest + rest * square * (
        -1.6666654611e-1 + square * (8.3321608736e-3 + square * -1.9515295891e-4)
    )
    cosine = (1.0 - 0.5 * square) + square * square * (
        4.166664568298827e-2 + square * (-1.388731625493765e-3 + square * 2.443315711809948e-5)
    )
    odd = (quadrant & 1) == 1
    swapped_sine = jnp.where(odd, cosine, sine)
    swapped_cosine = jnp.where(odd, sine, cosine)
    sine = jnp.where((quadrant & 2) == 2, -swapped_sine, swapped_sine)
    cosine = jnp.where(((quadrant + 1) & 2) == 2, -swapped_cosine, swapped_cosine)
    return sine, cosine


def kernel(
    levels,
    images_in,
    matrix,
    offsets_in,
    tap_index_in,
    tap_table_in,
    phase_base_in,
    phase_slope_in,
    out,
    images,
    offsets,
    tap_index,
    tap_table,
    phase_base,
    phase_slope,
    source,
    image,
    rows_of,
    params,
    trig,
    staging,
    outgoing,
    incoming,
    kept,
    windows,
    handed,
    assembled,
    local_sem,
    sent_sem,
    sibling_sem,
    inter_sem,
    merge_sem,
    last_sem,
):
    width = image.shape[2]
    angles = image.shape[3]
    span = images.shape[2]
    share = rows_of.shape[1]
    cores = angles // share
    tiles = share // LANES
    steps = width // REACH
    per_owner = span // REACH
    taps = tap_table.shape[0]
    scene = lax.axis_index("scene")
    aper = lax.axis_index("aper")
    core = lax.axis_index("range")
    other = 1 - core
    first_row = pl.multiple_of(core * share, share)
    other_row = pl.multiple_of(other * share, share)
    halves = [lax.rem(aper // 2**level, 2) for level in range(levels)]
    partners = [aper + (1 - 2 * halves[level]) * 2**level for level in range(levels)]

    barrier = pltpu.get_barrier_semaphore()
    for partner in partners:
        pl.semaphore_signal(barrier, inc=1, device_id=(scene, partner, core), device_id_type=MESH)
    pl.semaphore_signal(barrier, inc=1, device_id=(scene, aper, other), device_id_type=MESH)

    pl.semaphore_signal(
        barrier, inc=1, device_id=(scene, partners[0], other), device_id_type=MESH
    )

    local_copies = [
        pltpu.make_async_copy(images_in.at[0], images, local_sem.at[0]),
        pltpu.make_async_copy(matrix, rows_of, local_sem.at[1]),
        pltpu.make_async_copy(offsets_in, offsets, local_sem.at[2]),
        pltpu.make_async_copy(tap_index_in, tap_index, local_sem.at[3]),
        pltpu.make_async_copy(phase_base_in, phase_base, local_sem.at[4]),
        pltpu.make_async_copy(phase_slope_in, phase_slope, local_sem.at[5]),
        pltpu.make_async_copy(tap_table_in, tap_table, local_sem.at[6]),
    ]
    for copy in local_copies:
        copy.start()

    def frame(step):
        return pl.ds(pl.multiple_of((step + 1) * REACH, REACH), REACH)

    def plain(step):
        return pl.ds(pl.multiple_of(step * REACH, REACH), REACH)

    def owner_of(step):
        return step // per_owner

    def local_step(step):
        return lax.rem(step, per_owner)

    def sibling_copy(step):
        return pltpu.make_async_remote_copy(
            src_ref=staging.at[0, :, plain(local_step(step)), :],
            dst_ref=kept.at[0, :, frame(step), :],
            send_sem=sent_sem.at[2 * levels],
            recv_sem=sibling_sem.at[step],
            device_id=(scene, aper, other),
            device_id_type=MESH,
        )

    def first_copy(step, place):
        return pltpu.make_async_remote_copy(
            src_ref=staging.at[1 + place, :, plain(local_step(step)), :],
            dst_ref=incoming.at[0, :, frame(step), :],
            send_sem=sent_sem.at[0],
            recv_sem=inter_sem.at[0, step],
            device_id=(scene, partners[0], core if place == 0 else other),
            device_id_type=MESH,
        )

    def inter_copy(level, step):
        return pltpu.make_async_remote_copy(
            src_ref=outgoing.at[level - 1, :, plain(step), :],
            dst_ref=incoming.at[level, :, frame(step), :],
            send_sem=sent_sem.at[level],
            recv_sem=inter_sem.at[level, step],
            device_id=(scene, partners[level], core),
            device_id_type=MESH,
        )

    def product(both, row):
        return lax.dot_general(
            both, row, (((1,), (1,)), ((), ())), preferred_element_type=F32
        ).astype(BF16)

    def first_products(j):
        step = core * per_owner + j
        both = jnp.concatenate([source[part, plain(j), :] for part in range(2)], axis=0)
        mine = halves[0] * cores
        yours = (1 - halves[0]) * cores
        for place, block in enumerate((mine + other, yours + core, yours + other)):
            inter = product(both, rows_of[block])
            for part in range(2):
                staging[place, part, plain(j), :] = inter[part * REACH : (part + 1) * REACH]
        inter = product(both, rows_of[mine + core])
        for part in range(2):
            kept[0, part, frame(step), :] = inter[part * REACH : (part + 1) * REACH]

    local_copies[0].wait()
    for part in range(2):
        source[part] = images[part].T
    local_copies[1].wait()
    for j in range(EARLY):
        first_products(j)
    edge = jnp.zeros((2, REACH, share), BF16)
    for level in range(levels):
        for buffer in (incoming, kept):
            buffer[level, :, 0:REACH, :] = edge
            buffer[level, :, REACH + width : REACH + width + REACH, :] = edge

    pl.semaphore_wait(barrier, len(partners) + 2)

    @pl.loop(0, per_owner)
    def _(j):
        step = core * per_owner + j

        @pl.when(j >= EARLY)
        def _():
            first_products(j)

        @pl.when(core == 0)
        def _():
            for place in range(2):
                first_copy(step, place).start()

        sibling_copy(step).start()

    for copy in local_copies[2:]:
        copy.wait()

    def tables(level):
        half = halves[level]
        picked = pl.ds(pl.multiple_of(half * angles + core * share, LANES), share)
        index = tap_index[level, :, picked]
        weights = [jnp.zeros(index.shape, F32) for _ in range(taps)]
        for entry in range(tap_table.shape[1]):
            hit = index == entry
            for tap in range(taps):
                weights[tap] = jnp.where(hit, tap_table[tap, entry], weights[tap])
        base = phase_base[level, :, picked]
        slope = phase_slope[level, :, picked]
        lines = weights + [offsets[level, :, picked].astype(F32) + float(REACH - 3), base, slope]
        for row, line in enumerate(lines):
            for slot in range(2):
                role = half if slot == 0 else 1 - half
                params[level, slot, row : row + 1, :] = jnp.where(role == 0, line[0:1], line[1:2])
        for slot in range(2):
            for tile in range(tiles):
                columns = slice(tile * LANES, (tile + 1) * LANES)

                def line(row, count):
                    return jnp.broadcast_to(
                        params[level, slot, row : row + 1, columns], (count, LANES)
                    )

                fine = lax.broadcasted_iota(jnp.int32, (REACH, LANES), 0).astype(F32)
                coarse = (
                    lax.broadcasted_iota(jnp.int32, (steps, LANES), 0) * REACH
                ).astype(F32)
                near = sincos(line(taps + 2, REACH) * fine)
                far = sincos(line(taps + 1, steps) + line(taps + 2, steps) * coarse)
                for step in range(steps):
                    sine = jnp.broadcast_to(far[0][step : step + 1], (REACH, LANES))
                    cosine = jnp.broadcast_to(far[1][step : step + 1], (REACH, LANES))
                    place = pl.ds(step * REACH, REACH)
                    trig[level, slot, 0, place, columns] = sine * near[1] + cosine * near[0]
                    trig[level, slot, 1, place, columns] = cosine * near[1] - sine * near[0]

    for level in range(levels):
        tables(level)

    def merge_copy(level, step, row):
        place = image.at[
            level - 1, :, pl.ds(pl.multiple_of(step * REACH, REACH), REACH), pl.ds(row, share)
        ]
        return pltpu.make_async_remote_copy(
            src_ref=place,
            dst_ref=place,
            send_sem=sent_sem.at[levels + level - 1],
            recv_sem=merge_sem.at[level - 1, step],
            device_id=(scene, aper, other),
            device_id_type=MESH,
        )

    def last_copy(step, row):
        return pltpu.make_async_remote_copy(
            src_ref=handed.at[:, plain(step), :],
            dst_ref=assembled.at[:, plain(local_step(step)), pl.ds(row, share)],
            send_sem=sent_sem.at[2 * levels - 1],
            recv_sem=last_sem.at[step],
            device_id=(scene, aper, other),
            device_id_type=MESH,
        )

    def send(level, step):
        merge_copy(level, step, other_row).wait_recv()
        here = plain(step)
        both = jnp.concatenate([image[level - 1, part, here, :] for part in range(2)], axis=0)
        away = product(both, rows_of[(1 - halves[level]) * cores + core])
        home = product(both, rows_of[halves[level] * cores + core])
        for part in range(2):
            outgoing[level - 1, part, here, :] = away[part * REACH : (part + 1) * REACH]
            kept[level, part, frame(step), :] = home[part * REACH : (part + 1) * REACH]
        inter_copy(level, step).start()

    def term(level, slot, step, tile):
        buffer = kept if slot == 0 else incoming
        columns = slice(tile * LANES, (tile + 1) * LANES)

        def line(row, count):
            return jnp.broadcast_to(params[level, slot, row : row + 1, columns], (count, LANES))

        amount = line(taps, 2 * REACH).astype(jnp.int32)
        weights = [line(tap, REACH) for tap in range(taps)]
        sine, cosine = [trig[level, slot, which, plain(step), columns] for which in range(2)]
        shifted = []
        for part in range(2):
            value = buffer[
                level, part, pl.ds(pl.multiple_of(step * REACH, REACH), 3 * REACH), columns
            ].astype(F32)
            keep = 2 * REACH
            bit = REACH
            value = jnp.concatenate(
                [
                    jnp.where((amount & bit) == bit, value[bit:], value[:keep]),
                    value[keep : keep + FINE],
                ],
                axis=0,
            )
            while bit > FINE:
                bit //= 2
                keep = value.shape[0] - bit
                value = jnp.where((amount[:keep] & bit) == bit, value[bit:], value[:keep])
            while bit > 1:
                bit //= 2
                turned = pltpu.roll(value, value.shape[0] - bit, 0)
                value = jnp.where((amount[: value.shape[0]] & bit) == bit, turned, value)
            window = windows.at[tile, slot, part]
            window[...] = value
            total = weights[0] * value[:REACH]
            for tap in range(1, taps):
                total = total + weights[tap] * window[tap : tap + REACH, :]
            shifted.append(total)
        return (
            shifted[0] * cosine - shifted[1] * sine,
            shifted[0] * sine + shifted[1] * cosine,
        )

    def merge(level, step):
        def arrive(at):
            if level > 0:
                inter_copy(level, at).wait_recv()
            else:
                first_copy(at, 0).wait_recv()

                @pl.when(owner_of(at) != core)
                def _():
                    sibling_copy(at).wait_recv()

        if level > 0:

            @pl.when(step == 0)
            def _():
                arrive(0)

        @pl.when(step + 1 < steps)
        def _():
            arrive(step + 1)

        here = pl.ds(pl.multiple_of(step * REACH, REACH), REACH)
        for tile in range(tiles):
            terms = [term(level, slot, step, tile) for slot in range(2)]
            for part in range(2):
                total = terms[0][part] + terms[1][part]
                if level + 1 < levels:
                    columns = pl.ds(pl.multiple_of(first_row + tile * LANES, LANES), LANES)
                    image[level, part, here, columns] = total.astype(BF16)
                else:
                    value = total.astype(BF16)

                    @pl.when(owner_of(step) == core)
                    def _():
                        columns = pl.ds(pl.multiple_of(first_row + tile * LANES, LANES), LANES)
                        assembled[part, plain(local_step(step)), columns] = value

                    @pl.when(owner_of(step) != core)
                    def _():
                        handed[part, here, tile * LANES : (tile + 1) * LANES] = value
        if level + 1 < levels:
            merge_copy(level + 1, step, first_row).start()
        else:

            @pl.when(owner_of(step) != core)
            def _():
                last_copy(step, first_row).start()

    if WAIT_FIRST:
        first_copy(0, 0).wait_recv()

    @pl.when(core != 0)
    def _():
        @pl.loop(0, per_owner)
        def _(j):
            for place in range(2):
                first_copy(core * per_owner + j, place).start()

        sibling_copy(0).wait_recv()

    if not WAIT_FIRST:
        first_copy(0, 0).wait_recv()

    stages = [(merge, 0, MERGE_LAGS[0])]
    for level in range(1, levels):
        stages.append((send, level, SEND_LAGS[level]))
        if level > 1:
            stages.append((merge, level - 1, MERGE_LAGS[level - 1]))
    if SEND_FIRST:
        stages = [(merge, 0, MERGE_LAGS[0])]
        stages += [(send, level, SEND_LAGS[level]) for level in range(1, levels)]
        stages += [(merge, level, MERGE_LAGS[level]) for level in range(1, levels - 1)]
    stages.append((merge, levels - 1, MERGE_LAGS[levels - 1]))
    lag = MERGE_LAGS[levels - 1]

    @pl.loop(0, steps + lag)
    def _(tick):
        for stage, level, late in stages:
            sends = stage is send
            lead = LEADS[level] if sends else 0
            paired = PAIRED[level][0 if sends else 1]

            @pl.when((tick >= late - lead) & (tick < late + steps))
            def _():
                count = COUNTS[level] if sends else 0
                first = tick == late - lead
                low = jnp.maximum(count, tick - late)
                high = tick - late + 1
                if count:
                    low = jnp.where(first, 0, low)
                    high = jnp.where(first, count, high)
                if paired:
                    low = jnp.where(tick - late == steps - 1, steps, low)
                    high = jnp.where(tick - late == steps - 2, steps, high)
                if count or paired:

                    @pl.loop(low, high)
                    def _(step):
                        stage(level, step)

                else:
                    stage(level, tick - late)

    def turn(row):
        for part in range(2):
            out[0, part, pl.ds(row, share), :] = assembled[part, :, pl.ds(row, share)].T

    turn(first_row)

    @pl.loop(0, per_owner)
    def _(j):
        last_copy(core * per_owner + j, other_row).wait_recv()

    turn(other_row)

    def all_sent(ref, sem):
        pltpu.make_async_remote_copy(
            src_ref=ref,
            dst_ref=ref,
            send_sem=sent_sem.at[sem],
            recv_sem=last_sem.at[0],
            device_id=(scene, aper, other),
            device_id_type=MESH,
        ).wait_send()

    all_sent(staging.at[0], 2 * levels)
    all_sent(staging.at[pl.ds(1, 2)], 0)
    for level in range(1, levels):
        all_sent(outgoing.at[level - 1], level)
        all_sent(image.at[level - 1, :, :, pl.ds(first_row, share)], levels + level - 1)
    theirs = pl.ds(pl.multiple_of(other * span, span), span)
    all_sent(handed.at[:, theirs, :], 2 * levels - 1)


def body(images, interp_matrix, offsets, tap_index, tap_table, phase_base, phase_slope):
    cores = lax.axis_size("range")
    levels = offsets.shape[0]
    angles = images.shape[2]
    span = images.shape[3]
    width = span * cores
    share = angles // cores
    steps = width // REACH
    vmem = pl.BlockSpec(memory_space=pltpu.VMEM)
    anywhere = pl.BlockSpec(memory_space=pl.ANY)
    framed = width + 2 * REACH
    return pl.pallas_call(
        functools.partial(kernel, levels),
        out_shape=pltpu.VMEM(images.shape, images.dtype),
        in_specs=[
            anywhere,
            anywhere,
            anywhere,
            anywhere,
            anywhere,
            anywhere,
            anywhere,
        ],
        out_specs=vmem,
        scratch_shapes=[
            pltpu.VMEM(images.shape[1:], images.dtype),
            pltpu.VMEM(offsets.shape, offsets.dtype),
            pltpu.VMEM(tap_index.shape, tap_index.dtype),
            pltpu.SMEM(tap_table.shape[::-1], F32),
            pltpu.VMEM(phase_base.shape, F32),
            pltpu.VMEM(phase_slope.shape, F32),
            pltpu.VMEM((2, span, angles), BF16),
            pltpu.VMEM((levels - 1, 2, width, angles), BF16),
            pltpu.VMEM((2 * cores, share, angles), BF16),
            pltpu.VMEM((levels, 2, 16, share), F32),
            pltpu.VMEM((levels, 2, 2, width, share), F32),
            pltpu.VMEM((3, 2, span, share), BF16),
            pltpu.VMEM((levels - 1, 2, width, share), BF16),
            pltpu.VMEM((levels, 2, framed, share), BF16),
            pltpu.VMEM((levels, 2, framed, share), BF16),
            pltpu.VMEM((share // LANES, 2, 2, REACH + 2 * FINE, LANES), F32),
            pltpu.VMEM((2, width, share), BF16),
            pltpu.VMEM((2, span, angles), BF16),
            pltpu.SemaphoreType.DMA((7,)),
            pltpu.SemaphoreType.DMA((2 * levels + 1,)),
            pltpu.SemaphoreType.DMA((steps,)),
            pltpu.SemaphoreType.DMA((levels, steps)),
            pltpu.SemaphoreType.DMA((levels - 1, steps)),
            pltpu.SemaphoreType.DMA((steps,)),
        ],
        compiler_params=pltpu.CompilerParams(collective_id=0, has_side_effects=True),
    )(images, interp_matrix.reshape(2 * cores, share, angles), offsets, tap_index, tap_table.T, phase_base, phase_slope)


def solution(mesh):
    return jax.shard_map(
        body,
        mesh=mesh,
        in_specs=(P(("scene", "aper"), None, None, "range"), P(), P(), P(), P(), P(), P()),
        out_specs=P(("scene", "aper"), None, None, "range"),
        check_vma=False,
    )
```
